512 devices in a mesh: req: 32 (over y, x, core), tok: 16 (over z).
Axes of the slice: x: 4, y: 4, z: 16, core: 2. Of those that a mesh axis runs over, the one named last changes fastest.
Arguments:
- queries: bfloat16 [128, 4, 128, 1024], P('req', None, 'tok'), may hold values from -18 to 18
- keys: bfloat16 [128, 4, 128, 128], P('req', None, 'tok'), may hold values from -5 to 5
- values: bfloat16 [128, 4, 128, 128], P('req', None, 'tok'), may hold values from -4 to 4
- key_cache_pool: bfloat16 [2048, 128, 2048], P('req', None, 'tok'), may hold values from -4 to 4
- value_cache_pool: bfloat16 [2048, 128, 2048], P('req', None, 'tok'), may hold values from -4 to 4
- cached_len: int32 [128], replicated, may hold values from 3072 to 4096, as said below
- page_table: int32 [128, 32, 2], replicated, may hold values from 0 to 63, as said below
Outputs:
- attended: bfloat16 [128, 4, 128, 1024], P('req', None, 'tok')
- new_keys: bfloat16 [128, 4, 128, 128], P('req', None, 'tok')
The draws below stay inside these ranges and needn't reach their ends.
Inputs may be any that keep to these rules, and one draw needn't show every extreme that they name: `cached_len`: A whole number of pages. In every draw some request whose pages lie in other groups has 32 pages. `page_table`: exactly half of the requests keep all pages in their own group, in slots below 32; for each other request of group g, page p lies in group (g + 1 + p) mod 32 in a slot of 32 or more. No two live pages of requests of one lane share a group and slot. So at most 1 pages of one request lie in one other group, and every draw reaches it. Entries past a request's pages are not used.
All inputs are finite; a program needn't handle non-finite values.
Results may differ from the reference program's by a relative error of at most 0.008.
Values may be sent and summed in bfloat16 or wider, within the bound.
A program may use at most 64 MiB of HBM per device.

```python
import jax
import jax.numpy as jnp
from jax import lax

KEY_VALUE_HEADS = 4
HEAD_SIZE = 128
QUERY_GROUP = 8
PAGE_TOKENS = 128
PAGES_PER_REQ = 32
ADDED_TOKENS = 128
GROUP_REQUESTS = 4
REQUEST_TOTAL = 128
POOL_SLOTS = 64
N_REQ = 32


def request_law(key):
    ranking = jax.random.permutation(jax.random.fold_in(key, 11), REQUEST_TOTAL)
    spread = jax.random.randint(jax.random.fold_in(key, 12), (REQUEST_TOTAL,), 3 * PAGES_PER_REQ // 4, PAGES_PER_REQ + 1)
    page_counts = jnp.where(ranking < 4, PAGES_PER_REQ, spread)
    remote = ranking % 2 == 1
    return (page_counts.astype(jnp.int32), remote)


def draw_cached_len(key, part):
    page_counts, remote = request_law(key)
    return (page_counts * PAGE_TOKENS).astype(jnp.int32)


def draw_page_table(key, part):
    page_counts, remote = request_law(key)
    request_ids = jnp.arange(REQUEST_TOTAL, dtype=jnp.int32)
    group_ids = request_ids // GROUP_REQUESTS
    lane_ids = request_ids % GROUP_REQUESTS
    page_ids = jnp.arange(PAGES_PER_REQ, dtype=jnp.int32)
    home_scores = jax.random.randint(jax.random.fold_in(key, 13), (REQUEST_TOTAL, PAGES_PER_REQ), 0, 1 << 20) * PAGES_PER_REQ + page_ids[None, :]
    home_slot = jnp.argsort(home_scores, axis=1, stable=True).astype(jnp.int32)
    far_scores = jax.random.randint(jax.random.fold_in(key, 14), (N_REQ, GROUP_REQUESTS, PAGES_PER_REQ), 0, 1 << 20) * PAGES_PER_REQ + page_ids
    far_perm = jnp.argsort(far_scores, axis=-1, stable=True).astype(jnp.int32)
    holder = (group_ids[:, None] + 1 + page_ids[None, :]) % N_REQ
    far_slot = PAGES_PER_REQ + far_perm[holder, lane_ids[:, None], page_ids[None, :]]
    group_column = jnp.where(remote[:, None], holder, group_ids[:, None])
    slot_column = jnp.where(remote[:, None], far_slot, home_slot)
    return jnp.stack([group_column, slot_column], axis=-1).astype(jnp.int32)


def key_law(key):
    array_shape = (REQUEST_TOTAL, KEY_VALUE_HEADS, ADDED_TOKENS, HEAD_SIZE)
    base = jnp.clip(jax.random.normal(jax.random.fold_in(key, 21), array_shape, jnp.float32), -4.0, 4.0)
    return base


def draw_keys(key, part):
    base = key_law(key)
    return base.astype(jnp.bfloat16)


def draw_queries(key, part):
    array_shape = (REQUEST_TOTAL, KEY_VALUE_HEADS, ADDED_TOKENS, QUERY_GROUP * HEAD_SIZE)
    return jnp.clip(jax.random.normal(jax.random.fold_in(key, 31), array_shape, jnp.float32), -4.0, 4.0).astype(jnp.bfloat16)


def levels(key, shape, split, smallest, high):
    factor_of = 1.0
    for axis_at, parts in split:
        steps = jax.random.uniform(jax.random.fold_in(jax.random.fold_in(key, 6), axis_at), (parts,), jnp.float32, smallest / len(split), high / len(split))
        factor_of = factor_of * jnp.repeat(jnp.exp(steps), shape[axis_at] // parts).reshape((-1,) + (1,) * (len(shape) - 1 - axis_at))
    return factor_of


def bell_draw(rng, shape, scale, bound, shards=(), held_as=jnp.bfloat16):
    array = scale * jax.random.normal(rng, shape, jnp.float32)
    if shards:
        array = array * levels(rng, shape, shards, -0.22, 0.18)
    return jnp.clip(array, -bound, bound).astype(held_as)


def setup_inputs(seed: int = 0) -> dict:
    key_list = jax.random.split(jax.random.key(seed), 8)
    return {
        "queries": draw_queries(jax.random.fold_in(key_list[7], 71), 0),
        "keys": draw_keys(jax.random.fold_in(key_list[7], 71), 0),
        "values": bell_draw(key_list[2], (REQUEST_TOTAL, KEY_VALUE_HEADS, ADDED_TOKENS, HEAD_SIZE), 1.0, 4.0, ((0, 32), (2, 16))),
        "key_cache_pool": bell_draw(key_list[3], (N_REQ * POOL_SLOTS, PAGE_TOKENS, GROUP_REQUESTS * KEY_VALUE_HEADS * HEAD_SIZE), 1.0, 4.0, ((0, 32), (2, 16))),
        "value_cache_pool": bell_draw(key_list[4], (N_REQ * POOL_SLOTS, PAGE_TOKENS, GROUP_REQUESTS * KEY_VALUE_HEADS * HEAD_SIZE), 1.0, 4.0, ((0, 32), (2, 16))),
        "cached_len": draw_cached_len(jax.random.fold_in(key_list[7], 71), 0),
        "page_table": draw_page_table(jax.random.fold_in(key_list[7], 71), 0),
    }


THETA = 5000000.0
NEGATIVE = -1.0e30
FAR_AWAY = 1 << 30


def apply_rotary(vectors, token_positions):
    head_dim = vectors.shape[-1]
    half_dim = head_dim // 2
    inverse = THETA ** (-(jnp.arange(half_dim, dtype=jnp.float32) * 2.0 / head_dim))
    angles = token_positions.astype(jnp.float32)[..., None] * inverse
    cosine = jnp.cos(angles)
    sine_table = jnp.sin(angles)
    first_half = vectors[..., :half_dim]
    back_half = vectors[..., half_dim:]
    return jnp.concatenate([first_half * cosine - back_half * sine_table, back_half * cosine + first_half * sine_table], axis=-1)


def reference(queries, keys, values, key_cache_pool, value_cache_pool, cached_len, page_table):
    heads_per_group = queries.shape[-1] // HEAD_SIZE
    score_scale = HEAD_SIZE ** -0.5
    token_index = jnp.arange(ADDED_TOKENS, dtype=jnp.int32)
    token_positions = cached_len[:, None] + token_index[None, :]
    query_rotated = apply_rotary(queries.astype(jnp.float32).reshape(REQUEST_TOTAL, KEY_VALUE_HEADS, ADDED_TOKENS, heads_per_group, HEAD_SIZE), token_positions[:, None, :, None]).astype(jnp.bfloat16)
    new_keys = apply_rotary(keys.astype(jnp.float32), token_positions[:, None, :]).astype(jnp.bfloat16)
    key_page = jnp.arange(PAGES_PER_REQ * PAGE_TOKENS, dtype=jnp.int32) // PAGE_TOKENS

    def attend(request):
        lane_index = request % GROUP_REQUESTS
        slot_pool_rows = page_table[request, :, 0] * POOL_SLOTS + page_table[request, :, 1]
        page_total = cached_len[request] // PAGE_TOKENS

        def columns(slot_pool):
            selected_rows = slot_pool[slot_pool_rows].reshape(PAGES_PER_REQ, PAGE_TOKENS, GROUP_REQUESTS, KEY_VALUE_HEADS, HEAD_SIZE)
            selected_rows = lax.dynamic_index_in_dim(selected_rows, lane_index, axis=2, keepdims=False)
            return jnp.transpose(selected_rows, (2, 0, 1, 3)).reshape(KEY_VALUE_HEADS, PAGES_PER_REQ * PAGE_TOKENS, HEAD_SIZE)

        all_keys = jnp.concatenate([columns(key_cache_pool), new_keys[request]], axis=1)
        all_values = jnp.concatenate([columns(value_cache_pool), values[request]], axis=1)
        cache_place = jnp.where(key_page < page_total, -1, FAR_AWAY).astype(jnp.int32)
        key_place = jnp.concatenate([cache_place, token_index])
        scores = jnp.einsum("hqgd,hkd->hqgk", query_rotated[request].astype(jnp.float32), all_keys.astype(jnp.float32)) * score_scale
        visible = key_place[None, None, None, :] <= token_index[None, :, None, None]
        row_max = jnp.max(jnp.where(visible, scores, NEGATIVE), axis=-1, keepdims=True)
        weights = jnp.where(visible, jnp.exp(scores - row_max), 0.0)
        total_weight = jnp.sum(weights, axis=-1)
        rounded = weights.astype(jnp.bfloat16)
        value_sum = jnp.einsum("hqgk,hkd->hqgd", rounded.astype(jnp.float32), all_values.astype(jnp.float32))
        return (value_sum / total_weight[..., None]).astype(jnp.bfloat16).reshape(KEY_VALUE_HEADS, ADDED_TOKENS, heads_per_group * HEAD_SIZE)

    attended = lax.map(attend, jnp.arange(REQUEST_TOTAL, dtype=jnp.int32))
    return attended, new_keys
```

```python
import functools

import jax
import jax.numpy as jnp
import numpy as np
from jax import lax
from jax.experimental import pallas as pl
from jax.experimental.pallas import tpu as pltpu
from jax.sharding import PartitionSpec as P

THETA = 5000000.0
NEGATIVE = -1e30
MESH = pl.DeviceIdType.MESH
LOG2E = 1.4426950408889634


def exchange_kernel(
    sizes,
    table_ref,
    len_ref,
    freq_ref,
    q_ref,
    k_ref,
    v_ref,
    kpool_ref,
    vpool_ref,
    rows_out,
    pages_out,
    newk_out,
    pool_k,
    pool_v,
    send_pages,
    send_rows,
    cos_ref,
    sin_ref,
    pool_sem,
    own_sem,
    row_send,
    row_recv,
    page_send,
    page_recv,
):
    n_req, n_tok, lanes, heads, toks, group, dim = sizes
    g = lax.axis_index("req")
    z = lax.axis_index("tok")
    lane = z // heads
    pool_copies = [
        pltpu.make_async_copy(kpool_ref, pool_k, pool_sem.at[0]),
        pltpu.make_async_copy(vpool_ref, pool_v, pool_sem.at[1]),
    ]
    for c in pool_copies:
        c.start()

    barrier = pltpu.get_barrier_semaphore()

    @pl.loop(1, n_tok)
    def _(d):
        pl.semaphore_signal(
            barrier, inc=1, device_id=(g, lax.rem(z + d, n_tok)), device_id_type=MESH
        )

    @pl.loop(1, n_req)
    def _(d):
        pl.semaphore_signal(
            barrier, inc=1, device_id=(lax.rem(g + d, n_req), z), device_id_type=MESH
        )

    steps = lax.broadcasted_iota(jnp.int32, (toks, dim), 0)
    cols = lax.broadcasted_iota(jnp.int32, (toks, dim), 1)
    for r in range(lanes):
        first = len_ref[g * lanes + r] + z * toks
        angle = (first + steps).astype(jnp.float32) * freq_ref[0:1, :]
        cos_ref[r] = jnp.cos(angle)
        sine = jnp.sin(angle)
        sin_ref[r] = jnp.where(cols < dim // 2, -sine, sine)

    @pl.loop(0, n_tok)
    def _(m):
        r = m // heads
        cosine = cos_ref[r]
        sine = sin_ref[r]

        def rotate(x):
            return (x * cosine + pltpu.roll(x, dim // 2, 1) * sine).astype(jnp.bfloat16)

        for j in range(group):
            x = q_ref[m, :, j * dim : (j + 1) * dim].astype(jnp.float32)
            send_rows[m, :, j * dim : (j + 1) * dim] = rotate(x)
        key = rotate(k_ref[m].astype(jnp.float32))
        send_rows[m, :, group * dim : (group + 1) * dim] = key
        newk_out[m] = key
        send_rows[m, :, (group + 1) * dim : (group + 2) * dim] = v_ref[m]

    own = pltpu.make_async_copy(send_rows.at[z], rows_out.at[z], own_sem)
    own.start()
    pl.semaphore_wait(barrier, n_tok + n_req - 2)

    def row_copy(d):
        t = lax.rem(z + d, n_tok)
        return pltpu.make_async_remote_copy(
            src_ref=send_rows.at[t],
            dst_ref=rows_out.at[z],
            send_sem=row_send.at[d],
            recv_sem=row_recv.at[d],
            device_id=(g, t),
            device_id_type=MESH,
        )

    @pl.loop(1, n_tok)
    def _(d):
        row_copy(d).start()

    for c in pool_copies:
        c.wait()

    @pl.loop(1, n_req)
    def _(d):
        j = lax.rem(g + d, n_req)
        p = n_req - 1 - d
        slot = table_ref[p, 1, j * lanes + lane]
        slot = jnp.clip(slot, 0, pool_k.shape[0] - 1)
        send_pages[p, 0] = pool_k[slot]
        send_pages[p, 1] = pool_v[slot]

    def page_copy(p):
        j = lax.rem(g + n_req - 1 - p, n_req)
        return pltpu.make_async_remote_copy(
            src_ref=send_pages.at[p],
            dst_ref=pages_out.at[p],
            send_sem=page_send.at[p],
            recv_sem=page_recv.at[p],
            device_id=(j, z),
            device_id_type=MESH,
        )

    @pl.loop(0, n_req - 1)
    def _(p):
        page_copy(p).start()

    own.wait()

    @pl.loop(1, n_tok)
    def _(d):
        s = lax.rem(z + n_tok - d, n_tok)
        c = pltpu.make_async_remote_copy(
            src_ref=send_rows.at[s],
            dst_ref=rows_out.at[s],
            send_sem=row_send.at[d],
            recv_sem=row_recv.at[d],
            device_id=(g, lax.rem(z + d, n_tok)),
            device_id_type=MESH,
        )
        c.wait_send()
        c.wait_recv()

    @pl.loop(0, n_req - 1)
    def _(p):
        c = page_copy(p)
        c.wait_send()
        c.wait_recv()


def attend_block(q_ref, keys, values, m_ref, l_ref, acc_ref, factor, chunk, mask=None):
    rows = q_ref.shape[0]
    n_keys = keys.shape[0]
    lane_blocks = n_keys // 128
    for start in range(0, rows, chunk):
        at = slice(start, start + chunk)
        s = (
            lax.dot_general(
                q_ref[at], keys, (((1,), (1,)), ((), ())), preferred_element_type=jnp.float32
            )
            * factor
        )
        if mask is not None:
            s = jnp.where(mask, s, NEGATIVE)
        m_old = m_ref[at]
        m_new = jnp.maximum(m_old, jnp.max(s, axis=1, keepdims=True))
        m_ref[at] = m_new
        alpha = jnp.exp2(m_old - m_new)
        pieces = [jnp.exp2(s[:, i * 128 : (i + 1) * 128] - m_new) for i in range(lane_blocks)]
        total = pieces[0]
        for piece in pieces[1:]:
            total = total + piece
        l_ref[at] = l_ref[at] * alpha + total
        weights = jnp.concatenate([piece.astype(jnp.bfloat16) for piece in pieces], axis=1)
        acc_ref[at] = acc_ref[at] * alpha + jnp.dot(
            weights, values, preferred_element_type=jnp.float32
        )


def attend_kernel(
    sizes,
    table_ref,
    len_ref,
    rows_ref,
    pages_ref,
    kpool_ref,
    vpool_ref,
    out_ref,
    key_buf,
    value_buf,
    q_buf,
    m_ref,
    l_ref,
    acc_ref,
    sems,
):
    n_req, n_tok, lanes, heads, toks, group, dim = sizes
    page = key_buf.shape[1]
    limit = key_buf.shape[0]
    g = lax.axis_index("req")
    z = lax.axis_index("tok")
    request = g * lanes + z // heads
    count = len_ref[request] // page
    remote = table_ref[0, 0, request] != g

    def fetches(p):
        slot = jnp.clip(table_ref[p, 1, request], 0, kpool_ref.shape[0] - 1)
        return slot

    @pl.loop(0, count)
    def _(p):
        far = jnp.logical_and(remote, p < n_req - 1)

        @pl.when(far)
        def _():
            pltpu.make_async_copy(pages_ref.at[p, 0], key_buf.at[p], sems.at[0, p]).start()
            pltpu.make_async_copy(pages_ref.at[p, 1], value_buf.at[p], sems.at[1, p]).start()

        @pl.when(jnp.logical_not(far))
        def _():
            slot = fetches(p)
            pltpu.make_async_copy(kpool_ref.at[slot], key_buf.at[p], sems.at[0, p]).start()
            pltpu.make_async_copy(vpool_ref.at[slot], value_buf.at[p], sems.at[1, p]).start()

    def wait(p):
        pltpu.make_async_copy(pages_ref.at[0, 0], key_buf.at[p], sems.at[0, p]).wait()
        pltpu.make_async_copy(pages_ref.at[0, 1], value_buf.at[p], sems.at[1, p]).wait()

    added = n_tok * toks
    for j in range(group):
        x = rows_ref[:, :, j * dim : (j + 1) * dim].astype(jnp.float32)
        q_buf[j * added : (j + 1) * added] = x.reshape(added, dim).astype(jnp.bfloat16)
    m_ref[...] = jnp.full_like(m_ref, NEGATIVE)
    l_ref[...] = jnp.zeros_like(l_ref)
    acc_ref[...] = jnp.zeros_like(acc_ref)
    factor = dim ** (-0.5) * LOG2E
    run = functools.partial(
        attend_block, q_buf, m_ref=m_ref, l_ref=l_ref, acc_ref=acc_ref, factor=factor
    )

    def fresh(j):
        x = rows_ref[:, :, j * dim : (j + 1) * dim].astype(jnp.float32)
        return x.reshape(added, dim).astype(jnp.bfloat16)

    token = lax.broadcasted_iota(jnp.int32, (added, added), 0)
    place = lax.broadcasted_iota(jnp.int32, (added, added), 1)
    run(fresh(group), fresh(group + 1), chunk=added, mask=place <= token)

    step = 4

    @pl.loop(0, count // step)
    def _(b):
        for i in range(step):
            wait(b * step + i)
        run(
            key_buf[pl.ds(b * step, step)].reshape(step * page, dim),
            value_buf[pl.ds(b * step, step)].reshape(step * page, dim),
            chunk=256,
        )

    @pl.loop(count // step * step, count)
    def _(p):
        wait(p)
        run(key_buf[p], value_buf[p], chunk=256)

    for j in range(group):
        at = slice(j * added, (j + 1) * added)
        total = jnp.sum(l_ref[at], axis=1, keepdims=True)
        x = acc_ref[at] / total
        out_ref[:, :, j * dim : (j + 1) * dim] = x.reshape(n_tok, toks, dim).astype(jnp.bfloat16)


def return_kernel(sizes, in_ref, out_ref, own_sem, send_sem, recv_sem):
    n_req, n_tok, lanes, heads, toks, group, dim = sizes
    g = lax.axis_index("req")
    z = lax.axis_index("tok")
    own = pltpu.make_async_copy(in_ref.at[z], out_ref.at[z], own_sem)
    own.start()
    barrier = pltpu.get_barrier_semaphore()

    @pl.loop(1, n_tok)
    def _(d):
        pl.semaphore_signal(
            barrier, inc=1, device_id=(g, lax.rem(z + d, n_tok)), device_id_type=MESH
        )

    pl.semaphore_wait(barrier, n_tok - 1)

    @pl.loop(1, n_tok)
    def _(d):
        t = lax.rem(z + d, n_tok)
        pltpu.make_async_remote_copy(
            src_ref=in_ref.at[t],
            dst_ref=out_ref.at[z],
            send_sem=send_sem.at[d],
            recv_sem=recv_sem.at[d],
            device_id=(g, t),
            device_id_type=MESH,
        ).start()

    own.wait()

    @pl.loop(1, n_tok)
    def _(d):
        s = lax.rem(z + n_tok - d, n_tok)
        c = pltpu.make_async_remote_copy(
            src_ref=in_ref.at[s],
            dst_ref=out_ref.at[s],
            send_sem=send_sem.at[d],
            recv_sem=recv_sem.at[d],
            device_id=(g, lax.rem(z + d, n_tok)),
            device_id_type=MESH,
        )
        c.wait_send()
        c.wait_recv()


def per_device(queries, keys, values, key_cache_pool, value_cache_pool, cached_len, page_table):
    n_req = lax.axis_size("req")
    n_tok = lax.axis_size("tok")
    lanes, heads, toks, width = queries.shape
    dim = keys.shape[-1]
    group = width // dim
    slots, page = key_cache_pool.shape[:2]
    limit = page_table.shape[1]
    sizes = (n_req, n_tok, lanes, heads, toks, group, dim)
    table = jnp.transpose(page_table, (1, 2, 0))
    half = np.arange(dim // 2, dtype=np.float32)
    inverse = np.float32(THETA) ** (-(half * np.float32(2.0) / np.float32(dim)))
    freq = jnp.asarray(np.tile(inverse.astype(np.float32), 2).reshape(1, dim))
    smem = pl.BlockSpec(memory_space=pltpu.SMEM)
    vmem = pl.BlockSpec(memory_space=pltpu.VMEM)
    hbm = pl.BlockSpec(memory_space=pl.ANY)
    bf16 = jnp.bfloat16
    rows, pages, new_keys = pl.pallas_call(
        functools.partial(exchange_kernel, sizes),
        out_shape=(
            jax.ShapeDtypeStruct((n_tok, toks, width + 2 * dim), bf16),
            jax.ShapeDtypeStruct((n_req - 1, 2, page, dim), bf16),
            jax.ShapeDtypeStruct((n_tok, toks, dim), bf16),
        ),
        in_specs=[smem, smem, vmem, vmem, vmem, vmem, hbm, hbm],
        out_specs=(hbm, hbm, vmem),
        scratch_shapes=[
            pltpu.VMEM((slots, page, dim), bf16),
            pltpu.VMEM((slots, page, dim), bf16),
            pltpu.VMEM((n_req - 1, 2, page, dim), bf16),
            pltpu.VMEM((n_tok, toks, width + 2 * dim), bf16),
            pltpu.VMEM((lanes, toks, dim), jnp.float32),
            pltpu.VMEM((lanes, toks, dim), jnp.float32),
            pltpu.SemaphoreType.DMA((2,)),
            pltpu.SemaphoreType.DMA,
            pltpu.SemaphoreType.DMA((n_tok,)),
            pltpu.SemaphoreType.DMA((n_tok,)),
            pltpu.SemaphoreType.DMA((n_req - 1,)),
            pltpu.SemaphoreType.DMA((n_req - 1,)),
        ],
        compiler_params=pltpu.CompilerParams(collective_id=0, has_side_effects=True),
        name="exchange_in",
    )(
        table,
        cached_len,
        freq,
        queries.reshape(n_tok, toks, width),
        keys.reshape(n_tok, toks, dim),
        values.reshape(n_tok, toks, dim),
        key_cache_pool,
        value_cache_pool,
    )
    added = n_tok * toks
    attended = pl.pallas_call(
        functools.partial(attend_kernel, sizes),
        out_shape=jax.ShapeDtypeStruct((n_tok, toks, width), bf16),
        in_specs=[smem, smem, vmem, hbm, hbm, hbm],
        out_specs=vmem,
        scratch_shapes=[
            pltpu.VMEM((limit, page, dim), bf16),
            pltpu.VMEM((limit, page, dim), bf16),
            pltpu.VMEM((added * group, dim), bf16),
            pltpu.VMEM((added * group, dim), jnp.float32),
            pltpu.VMEM((added * group, dim), jnp.float32),
            pltpu.VMEM((added * group, dim), jnp.float32),
            pltpu.SemaphoreType.DMA((2, limit)),
        ],
        name="attend",
    )(table, cached_len, rows, pages, key_cache_pool, value_cache_pool)
    returned = pl.pallas_call(
        functools.partial(return_kernel, sizes),
        out_shape=jax.ShapeDtypeStruct((n_tok, toks, width), bf16),
        in_specs=[vmem],
        out_specs=vmem,
        scratch_shapes=[
            pltpu.SemaphoreType.DMA,
            pltpu.SemaphoreType.DMA((n_tok,)),
            pltpu.SemaphoreType.DMA((n_tok,)),
        ],
        compiler_params=pltpu.CompilerParams(collective_id=1, has_side_effects=True),
        name="exchange_out",
    )(attended)
    return (
        returned.reshape(lanes, heads, toks, width),
        new_keys.reshape(lanes, heads, toks, dim),
    )


def solution(mesh):
    placed = (
        P("req", None, "tok", None),
        P("req", None, "tok", None),
        P("req", None, "tok", None),
        P("req", None, "tok"),
        P("req", None, "tok"),
        P(),
        P(),
    )
    return jax.shard_map(
        per_device,
        mesh=mesh,
        in_specs=placed,
        out_specs=(P("req", None, "tok", None), P("req", None, "tok", None)),
        check_vma=False,
    )
```

```python
import functools

import jax
import jax.numpy as jnp
import numpy as np
from jax import lax
from jax.experimental import pallas as pl
from jax.experimental.pallas import tpu as pltpu
from jax.sharding import PartitionSpec as P

THETA = 5000000.0
NEGATIVE = -1e30
MESH = pl.DeviceIdType.MESH
LOG2E = 1.4426950408889634
RING_Y, RING_X, CORES = 4, 4, 2
STEP = 4
CHUNK = 512


def ring_distance(d, n):
    return min(d % n, n - d % n)


PARTNERS = sorted(
    [
        (dy, dx, dc)
        for dy in range(RING_Y)
        for dx in range(RING_X)
        for dc in range(CORES)
        if (dy, dx, dc) != (0, 0, 0)
    ],
    key=lambda o: -(ring_distance(o[0], RING_Y) + ring_distance(o[1], RING_X)),
)


def tok_order(n):
    return sorted(range(1, n), key=lambda d: -ring_distance(d, n))


def partner(g, offset, sign):
    dy, dx, dc = offset
    c = lax.rem(g, CORES)
    x = lax.rem(g // CORES, RING_X)
    y = g // (CORES * RING_X)
    y = lax.rem(y + sign * dy + RING_Y, RING_Y)
    x = lax.rem(x + sign * dx + RING_X, RING_X)
    c = lax.rem(c + dc, CORES)
    return (y * RING_X + x) * CORES + c


def layer_kernel(
    sizes,
    table_ref,
    len_ref,
    freq_ref,
    q_hbm,
    k_hbm,
    v_hbm,
    kpool_ref,
    vpool_ref,
    out_ref,
    newk_out,
    q_in,
    k_in,
    v_in,
    newk,
    pool_k,
    pool_v,
    send_pages,
    recv_pages,
    send_rows,
    recv_rows,
    out_rows,
    cos_ref,
    sin_ref,
    page_ids,
    q_buf,
    fill,
    key_blk,
    value_t,
    s_buf,
    m_ref,
    m_old_ref,
    alpha_ref,
    l_ref,
    acc_ref,
    in_sem,
    pool_sem,
    newk_sem,
    own_sem,
    row_send,
    row_recv,
    page_send,
    page_recv,
    out_send,
    out_recv,
):
    n_req, n_tok, lanes, heads, toks, group, dim = sizes
    added = n_tok * toks
    rows = added * group
    page = pool_k.shape[1]
    n_far = n_req - 1
    factor = dim ** (-0.5) * LOG2E
    g = lax.axis_index("req")
    z = lax.axis_index("tok")
    lane = z // heads
    request = g * lanes + lane

    in_copies = [
        pltpu.make_async_copy(src, dst, in_sem.at[i])
        for i, (src, dst) in enumerate(((q_hbm, q_in), (k_hbm, k_in), (v_hbm, v_in)))
    ]
    pool_copies = [
        pltpu.make_async_copy(kpool_ref, pool_k, pool_sem.at[0]),
        pltpu.make_async_copy(vpool_ref, pool_v, pool_sem.at[1]),
    ]
    for c in in_copies:
        c.start()
    for c in pool_copies:
        c.start()

    barrier = pltpu.get_barrier_semaphore()
    z_order = tok_order(n_tok)
    for d in z_order:
        pl.semaphore_signal(
            barrier, inc=1, device_id=(g, lax.rem(z + d, n_tok)), device_id_type=MESH
        )
    for offset in PARTNERS:
        pl.semaphore_signal(
            barrier, inc=1, device_id=(partner(g, offset, 1), z), device_id_type=MESH
        )

    for k, offset in enumerate(PARTNERS):
        page_ids[k] = lax.rem(partner(g, offset, -1) + n_req - g + n_req - 1, n_req)
    page_ids[n_far] = n_req - 1

    steps = lax.broadcasted_iota(jnp.int32, (toks, dim), 0)
    cols = lax.broadcasted_iota(jnp.int32, (toks, dim), 1)
    for r in range(lanes):
        first = len_ref[g * lanes + r] + z * toks
        angle = (first + steps).astype(jnp.float32) * freq_ref[0:1, :]
        cos_ref[r] = jnp.cos(angle)
        sine = jnp.sin(angle)
        sin_ref[r] = jnp.where(cols < dim // 2, -sine, sine)

    for c in in_copies:
        c.wait()

    @pl.loop(0, n_tok)
    def _(m):
        r = m // heads
        cosine = cos_ref[r]
        sine = sin_ref[r]

        def rotate(x):
            return (x * cosine + pltpu.roll(x, dim // 2, 1) * sine).astype(jnp.bfloat16)

        for j in range(group):
            x = q_in[m, :, j * dim : (j + 1) * dim].astype(jnp.float32)
            send_rows[m, :, j * dim : (j + 1) * dim] = rotate(x)
        key = rotate(k_in[m].astype(jnp.float32))
        send_rows[m, :, group * dim : (group + 1) * dim] = key
        newk[m] = key
        send_rows[m, :, (group + 1) * dim : (group + 2) * dim] = v_in[m]

    newk_copy = pltpu.make_async_copy(newk, newk_out, newk_sem)
    newk_copy.start()
    for c in pool_copies:
        c.wait()

    def slot_of(p, r):
        return jnp.clip(table_ref[p, 1, r], 0, pool_k.shape[0] - 1)

    for k, offset in enumerate(PARTNERS):
        j = partner(g, offset, 1)
        slot = slot_of(lax.rem(g + n_req - j + n_req - 1, n_req), j * lanes + lane)
        send_pages[k, 0] = pool_k[slot]
        send_pages[k, 1] = pool_v[slot]

    recv_rows[z] = send_rows[z]
    pl.semaphore_wait(barrier, n_tok + n_req - 2)

    def row_copy(d):
        t = lax.rem(z + d, n_tok)
        return pltpu.make_async_remote_copy(
            src_ref=send_rows.at[t],
            dst_ref=recv_rows.at[z],
            send_sem=row_send.at[d],
            recv_sem=row_recv.at[d],
            device_id=(g, t),
            device_id_type=MESH,
        )

    def page_copy(k):
        return pltpu.make_async_remote_copy(
            src_ref=send_pages.at[k],
            dst_ref=recv_pages.at[k],
            send_sem=page_send.at[k],
            recv_sem=page_recv.at[k],
            device_id=(partner(g, PARTNERS[k], 1), z),
            device_id_type=MESH,
        )

    for d in z_order:
        row_copy(d).start()
    for k in range(n_far):
        page_copy(k).start()

    def wait_row(d):
        s = lax.rem(z + n_tok - d, n_tok)
        pltpu.make_async_remote_copy(
            src_ref=send_rows.at[s],
            dst_ref=recv_rows.at[s],
            send_sem=row_send.at[d],
            recv_sem=row_recv.at[d],
            device_id=(g, lax.rem(z + d, n_tok)),
            device_id_type=MESH,
        ).wait_recv()

    def wait_page(k):
        pltpu.make_async_remote_copy(
            src_ref=send_pages.at[k],
            dst_ref=recv_pages.at[k],
            send_sem=page_send.at[k],
            recv_sem=page_recv.at[k],
            device_id=(lax.rem(g + 1, n_req), z),
            device_id_type=MESH,
        ).wait_recv()

    count = len_ref[request] // page
    remote = table_ref[0, 0, request] != g

    @pl.loop(1, n_tok)
    def _(d):
        wait_row(d)

    def columns(j):
        x = recv_rows[:, :, j * dim : (j + 1) * dim].astype(jnp.float32)
        return x.reshape(added, dim)

    for j in range(group):
        q_buf[j * added : (j + 1) * added] = columns(j).astype(jnp.bfloat16)
    fresh_k = columns(group)
    fresh_v = columns(group + 1)
    fill[...] = jnp.broadcast_to(fresh_k[0:1, :], (page, dim)).astype(jnp.bfloat16)

    m_ref[...] = jnp.full_like(m_ref, NEGATIVE)
    l_ref[...] = jnp.zeros_like(l_ref)
    acc_ref[...] = jnp.zeros_like(acc_ref)

    def put_page(slot, i, live, keys, values):
        at = slice(i * page, (i + 1) * page)
        key_blk[slot, at] = jnp.where(live, keys, fill[...])
        value_t[slot, :, at] = jnp.where(live, values, jnp.zeros_like(values)).T

    def live_page(k):
        return page_ids[k] < count

    def stage(first, n, slot):
        for i in range(n):
            k = first + i
            wait_page(k)
            at = slot_of(page_ids[k], request)
            keys = jnp.where(remote, recv_pages[k, 0], pool_k[at])
            values = jnp.where(remote, recv_pages[k, 1], pool_v[at])
            put_page(slot, i, live_page(k), keys, values)

    chunks = range(0, rows, CHUNK)

    def score(slot, n, c0, mask=None):
        at = slice(c0, c0 + CHUNK)
        s = lax.dot_general(
            key_blk[slot, : n * page],
            q_buf[at],
            (((1,), (1,)), ((), ())),
            preferred_element_type=jnp.float32,
        )
        if mask is not None:
            s = jnp.where(mask, s, NEGATIVE)
        s_buf[slot, : n * page, at] = s
        m_old = m_ref[:, at]
        m_new = jnp.maximum(m_old, jnp.max(s, axis=0, keepdims=True))
        m_ref[:, at] = m_new
        m_old_ref[slot, :, at] = m_new
        alpha_ref[slot, :, at] = jnp.exp2((m_old - m_new) * factor)

    def gather(slot, n, c0, lives):
        at = slice(c0, c0 + CHUNK)
        weights = jnp.exp2((s_buf[slot, : n * page, at] - m_old_ref[slot, :, at]) * factor)
        alpha = alpha_ref[slot, :, at]
        total = l_ref[:, at] * alpha
        for i in range(n):
            part = weights[i * page : (i + 1) * page].reshape(page // 8, 8, CHUNK)
            part = jnp.sum(part, axis=0)
            if lives[i] is not None:
                part = part * lives[i].astype(jnp.float32)
            total = total + part
        l_ref[:, at] = total
        acc_ref[:, at] = acc_ref[:, at] * alpha + jnp.dot(
            value_t[slot, :, : n * page],
            weights.astype(jnp.bfloat16),
            preferred_element_type=jnp.float32,
        )

    def lives_of(first, n):
        return [live_page(first + i) for i in range(n)]

    key_blk[0, :page] = fresh_k.astype(jnp.bfloat16)
    value_t[0, :, :page] = fresh_v.T.astype(jnp.bfloat16)
    own_slot = slot_of(n_req - 1, request)
    put_page(0, 1, live_page(n_far), pool_k[own_slot], pool_v[own_slot])
    place = lax.broadcasted_iota(jnp.int32, (2 * page, CHUNK), 0)
    token = lax.rem(lax.broadcasted_iota(jnp.int32, (2 * page, CHUNK), 1), added)
    visible = jnp.logical_or(place <= token, place >= page)
    for c0 in chunks:
        score(0, 2, c0, visible)
    stage(0, STEP, 1)
    for c0 in chunks:
        score(1, STEP, c0)
        gather(0, 2, c0, [None, live_page(n_far)])

    full = n_far // STEP
    tail = n_far - full * STEP
    pairs = (full - 1) // 2

    @pl.loop(0, pairs)
    def _(b):
        for i in range(2):
            first = (2 * b + i + 1) * STEP
            stage(first, STEP, i)
            for c0 in chunks:
                score(i, STEP, c0)
                gather(1 - i, STEP, c0, lives_of(first - STEP, STEP))

    last = full * STEP
    stage(last, tail, 0)
    for c0 in chunks:
        score(0, tail, c0)
        gather(1, STEP, c0, lives_of(last - STEP, STEP))
    for c0 in chunks:
        gather(0, tail, c0, lives_of(last, tail))

    total = jnp.sum(l_ref[...], axis=0, keepdims=True)
    for j in range(group):
        at = slice(j * added, (j + 1) * added)
        x = (acc_ref[:, at] / total[:, at]).T
        out_rows[:, :, j * dim : (j + 1) * dim] = x.reshape(n_tok, toks, dim).astype(jnp.bfloat16)

    def out_copy(d):
        t = lax.rem(z + d, n_tok)
        return pltpu.make_async_remote_copy(
            src_ref=out_rows.at[t],
            dst_ref=out_ref.at[z],
            send_sem=out_send.at[d],
            recv_sem=out_recv.at[d],
            device_id=(g, t),
            device_id_type=MESH,
        )

    for d in z_order:
        out_copy(d).start()
    own = pltpu.make_async_copy(out_rows.at[z], out_ref.at[z], own_sem)
    own.start()

    @pl.loop(1, n_tok)
    def _(d):
        row_copy(d).wait_send()

    for k in range(n_far):
        page_copy(k).wait_send()
    newk_copy.wait()
    own.wait()

    @pl.loop(1, n_tok)
    def _(d):
        s = lax.rem(z + n_tok - d, n_tok)
        c = pltpu.make_async_remote_copy(
            src_ref=out_rows.at[s],
            dst_ref=out_ref.at[s],
            send_sem=out_send.at[d],
            recv_sem=out_recv.at[d],
            device_id=(g, lax.rem(z + d, n_tok)),
            device_id_type=MESH,
        )
        c.wait_send()
        c.wait_recv()


def per_device(queries, keys, values, key_cache_pool, value_cache_pool, cached_len, page_table):
    n_req = lax.axis_size("req")
    n_tok = lax.axis_size("tok")
    lanes, heads, toks, width = queries.shape
    dim = keys.shape[-1]
    group = width // dim
    slots, page = key_cache_pool.shape[:2]
    sizes = (n_req, n_tok, lanes, heads, toks, group, dim)
    rows = n_tok * toks * group
    table = jnp.transpose(page_table, (1, 2, 0))
    half = np.arange(dim // 2, dtype=np.float32)
    inverse = np.float32(THETA) ** (-(half * np.float32(2.0) / np.float32(dim)))
    freq = jnp.asarray(np.tile(inverse.astype(np.float32), 2).reshape(1, dim))
    smem = pl.BlockSpec(memory_space=pltpu.SMEM)
    vmem = pl.BlockSpec(memory_space=pltpu.VMEM)
    hbm = pl.BlockSpec(memory_space=pl.ANY)
    bf16, f32 = jnp.bfloat16, jnp.float32
    dma = pltpu.SemaphoreType.DMA
    returned, new_keys = pl.pallas_call(
        functools.partial(layer_kernel, sizes),
        out_shape=(
            jax.ShapeDtypeStruct((n_tok, toks, width), bf16),
            jax.ShapeDtypeStruct((n_tok, toks, dim), bf16),
        ),
        in_specs=[smem, smem, vmem, hbm, hbm, hbm, hbm, hbm],
        out_specs=(hbm, hbm),
        scratch_shapes=[
            pltpu.VMEM((n_tok, toks, width), bf16),
            pltpu.VMEM((n_tok, toks, dim), bf16),
            pltpu.VMEM((n_tok, toks, dim), bf16),
            pltpu.VMEM((n_tok, toks, dim), bf16),
            pltpu.VMEM((slots, page, dim), bf16),
            pltpu.VMEM((slots, page, dim), bf16),
            pltpu.VMEM((n_req - 1, 2, page, dim), bf16),
            pltpu.VMEM((n_req - 1, 2, page, dim), bf16),
            pltpu.VMEM((n_tok, toks, width + 2 * dim), bf16),
            pltpu.VMEM((n_tok, toks, width + 2 * dim), bf16),
            pltpu.VMEM((n_tok, toks, width), bf16),
            pltpu.VMEM((lanes, toks, dim), f32),
            pltpu.VMEM((lanes, toks, dim), f32),
            pltpu.SMEM((n_req,), jnp.int32),
            pltpu.VMEM((rows, dim), bf16),
            pltpu.VMEM((page, dim), bf16),
            pltpu.VMEM((2, STEP * page, dim), bf16),
            pltpu.VMEM((2, dim, STEP * page), bf16),
            pltpu.VMEM((2, STEP * page, rows), f32),
            pltpu.VMEM((1, rows), f32),
            pltpu.VMEM((2, 1, rows), f32),
            pltpu.VMEM((2, 1, rows), f32),
            pltpu.VMEM((8, rows), f32),
            pltpu.VMEM((dim, rows), f32),
            dma((3,)),
            dma((2,)),
            dma,
            dma,
            dma((n_tok,)),
            dma((n_tok,)),
            dma((n_req - 1,)),
            dma((n_req - 1,)),
            dma((n_tok,)),
            dma((n_tok,)),
        ],
        compiler_params=pltpu.CompilerParams(collective_id=0, has_side_effects=True),
        name="layer",
    )(
        table,
        cached_len,
        freq,
        queries.reshape(n_tok, toks, width),
        keys.reshape(n_tok, toks, dim),
        values.reshape(n_tok, toks, dim),
        key_cache_pool,
        value_cache_pool,
    )
    return (
        returned.reshape(lanes, heads, toks, width),
        new_keys.reshape(lanes, heads, toks, dim),
    )


def solution(mesh):
    placed = (
        P("req", None, "tok", None),
        P("req", None, "tok", None),
        P("req", None, "tok", None),
        P("req", None, "tok"),
        P("req", None, "tok"),
        P(),
        P(),
    )
    return jax.shard_map(
        per_device,
        mesh=mesh,
        in_specs=placed,
        out_specs=(P("req", None, "tok", None), P("req", None, "tok", None)),
        check_vma=False,
    )
```
